32 devices in a mesh: pb: 4 (over y, core), kv: 8 (over z, x).
Axes of the slice: x: 2, y: 2, z: 4, core: 2. Of those that a mesh axis runs over, the one named last changes fastest.
Arguments:
- queries: bfloat16 [8192, 128], P(('pb', 'kv')), may hold values from -15 to 15
- query_tangent: bfloat16 [8192, 128], P(('pb', 'kv')), may hold values from -2 to 2
- keys: bfloat16 [8192, 128], P(('pb', 'kv')), may hold values from -8 to 8
- values: bfloat16 [8192, 128], P(('pb', 'kv')), may hold values from -6 to 6
- key_tangent: bfloat16 [8192, 128], P(('pb', 'kv')), may hold values from -2 to 2
- value_tangent: bfloat16 [8192, 128], P(('pb', 'kv')), may hold values from -6 to 6
- block_list: int32 [64, 8, 8], P('pb', 'kv'), may hold values from 0 to 63, as said below
- block_count: int32 [64, 8], P('pb', 'kv'), may hold values from 1 to 8, as said below
Outputs:
- attended: bfloat16 [8192, 128], P(('pb', 'kv'))
- attended_tangent: bfloat16 [8192, 128], P(('pb', 'kv'))
The draws below stay inside these ranges and needn't reach their ends.
Inputs may be any that keep to these rules, and one draw needn't show every extreme that they name: `block_list`: entries for one query block and slab j are distinct key blocks g whose index g // (256 // 128) leaves remainder j when divided by 8; entries past block_count are valid but unused. `block_count`: the value 8 is reached in every key slab.
All inputs are finite; a program needn't handle non-finite values.
Results may differ from the reference program's by a relative error of at most 0.01.
Values may be sent and summed in bfloat16 or wider, within the bound.
A program may use at most 128 MiB of HBM per device.

```python
import math
import jax
import jax.numpy as jnp
from jax import lax

HD = 128
BLK = 128
LMAX = 8
TOK_DEV = 256
SEQ = 8192
QBLOCKS = 64
KSLABS = 8


def draw_queries(key, part):
    result = jnp.clip(2.5 * jax.random.normal(key, (SEQ, HD), jnp.float32), -15.0, 15.0)
    return result.astype(jnp.bfloat16)


def draw_keys(key, part):
    noise = jax.random.normal(jax.random.fold_in(key, 3), (SEQ, HD), jnp.float32)
    result = jnp.clip(noise, -6.0, 6.0)
    return result.astype(jnp.bfloat16)


def block_tables(key):
    base = jax.random.fold_in(key, 7)
    level_key, raw_key, force_key, order_key = jax.random.split(base, 4)
    slab_blocks = SEQ // (BLK * KSLABS)
    shard_blocks = TOK_DEV // BLK
    per_query_slab = QBLOCKS // (SEQ // (TOK_DEV * KSLABS))
    level = jax.random.randint(level_key, (SEQ // (TOK_DEV * KSLABS), KSLABS), 1, LMAX + 1)
    row_level = jnp.repeat(level, per_query_slab, axis=0)
    raw = jax.random.randint(raw_key, (QBLOCKS, KSLABS), 0, 1 << 20)
    counts = 1 + raw % row_level
    forced = jax.random.randint(force_key, (KSLABS,), 0, QBLOCKS)
    counts = jnp.where(jnp.arange(QBLOCKS)[:, None] == forced[None, :], LMAX, counts)
    ranks = jax.random.randint(order_key, (QBLOCKS, KSLABS, slab_blocks), 0, 1 << 20)
    ranks = ranks * slab_blocks + jnp.arange(slab_blocks)[None, None, :]
    picked = jnp.argsort(ranks, axis=-1, stable=True)[:, :, :LMAX]
    slab_index = jnp.arange(KSLABS)[None, :, None]
    global_block = (picked // shard_blocks * KSLABS + slab_index) * shard_blocks + picked % shard_blocks
    return (global_block.astype(jnp.int32), counts.astype(jnp.int32))


def draw_block_list(key, part):
    return block_tables(key)[0]


def draw_block_count(key, part):
    return block_tables(key)[1]


def steps_of(stream_key, dims, pieces, least, largest):
    def one(axis_at, parts):
        steps = jax.random.uniform(jax.random.fold_in(jax.random.fold_in(stream_key, 6), axis_at), (parts,), jnp.float32, least / len(pieces), largest / len(pieces))
        return jnp.repeat(jnp.exp(steps), dims[axis_at] // parts).reshape((-1,) + (1,) * (len(dims) - axis_at - 1))

    gain = one(*pieces[0])
    for cut in pieces[1:]:
        gain = gain * one(*cut)
    return gain


def bell_draw(stream_key, dims, deviation, limit, pieces=(), kind=jnp.bfloat16):
    values = jax.random.normal(stream_key, dims, jnp.float32) * deviation
    if len(pieces) > 0:
        values = steps_of(stream_key, dims, pieces, -0.22, 0.18) * values
    return jnp.clip(values, min=-limit, max=limit).astype(kind)


def setup_inputs(seed: int = 0) -> dict:
    streams_of = jax.random.split(jax.random.key(seed), 9)
    return {
        "queries": draw_queries(jax.random.fold_in(streams_of[8], 71), 0),
        "query_tangent": bell_draw(streams_of[1], (SEQ, HD), 0.3, 2.0, ((0, 32),)),
        "keys": draw_keys(jax.random.fold_in(streams_of[8], 71), 0),
        "values": bell_draw(streams_of[3], (SEQ, HD), 1.0, 6.0, ((0, 32),)),
        "key_tangent": bell_draw(streams_of[4], (SEQ, HD), 0.3, 2.0, ((0, 32),)),
        "value_tangent": bell_draw(streams_of[5], (SEQ, HD), 1.0, 6.0, ((0, 32),)),
        "block_list": draw_block_list(jax.random.fold_in(streams_of[8], 71), 0),
        "block_count": draw_block_count(jax.random.fold_in(streams_of[8], 71), 0),
    }


def reference(queries, query_tangent, keys, values, key_tangent, value_tangent, block_list, block_count):
    score_scale = 1.0 / math.sqrt(HD)
    key_blocks = keys.reshape(QBLOCKS, BLK, HD)
    value_blocks = values.reshape(QBLOCKS, BLK, HD)
    keyt_blocks = key_tangent.reshape(QBLOCKS, BLK, HD)
    valuet_blocks = value_tangent.reshape(QBLOCKS, BLK, HD)

    def one_block(items):
        query_block, tangent_block, picked, counts = items
        flat = picked.reshape(-1)
        key_rows = key_blocks[flat].reshape(-1, HD)
        value_rows = value_blocks[flat].reshape(-1, HD)
        keyt_rows = keyt_blocks[flat].reshape(-1, HD)
        valuet_rows = valuet_blocks[flat].reshape(-1, HD)
        active = jnp.repeat((jnp.arange(LMAX)[None, :] < counts[:, None]).reshape(-1), BLK)
        scores = jnp.dot(query_block, key_rows.T, preferred_element_type=jnp.float32) * score_scale
        score_tangent = (jnp.dot(tangent_block, key_rows.T, preferred_element_type=jnp.float32) + jnp.dot(query_block, keyt_rows.T, preferred_element_type=jnp.float32)) * score_scale
        peak = lax.optimization_barrier(jnp.max(jnp.where(active[None, :], scores, -jnp.inf), axis=1))
        weights = jnp.where(active[None, :], jnp.exp(scores - peak[:, None]), 0.0)
        total = lax.optimization_barrier(jnp.sum(weights, axis=1))
        slope = lax.optimization_barrier(jnp.sum(weights * score_tangent, axis=1))
        weights_b = weights.astype(jnp.bfloat16)
        scaled_b = (weights * score_tangent).astype(jnp.bfloat16)
        weighted = jnp.dot(weights_b, value_rows, preferred_element_type=jnp.float32)
        tangent_sum = jnp.dot(scaled_b, value_rows, preferred_element_type=jnp.float32) + jnp.dot(weights_b, valuet_rows, preferred_element_type=jnp.float32)
        output = weighted / total[:, None]
        output_tangent = tangent_sum / total[:, None] - (slope / total)[:, None] * output
        return (output.astype(jnp.bfloat16), output_tangent.astype(jnp.bfloat16))
    query_blocks = queries.reshape(QBLOCKS, BLK, HD)
    tangent_blocks = query_tangent.reshape(QBLOCKS, BLK, HD)
    attended, attended_tangent = lax.map(one_block, (query_blocks, tangent_blocks, block_list, block_count))
    return (attended.reshape(SEQ, HD), attended_tangent.reshape(SEQ, HD))
```

```python
import functools
import math

import jax
import jax.numpy as jnp
from jax import lax
from jax.experimental import pallas as pl
from jax.experimental.pallas import tpu as pltpu
from jax.sharding import PartitionSpec as P

BLK = 128
NT = (((1,), (1,)), ((), ()))
MESH = pl.DeviceIdType.MESH


def flip(a, b, bits):
    out = 0
    for k in range(bits):
        w = 1 << k
        out = out + (a // w + b // w) % 2 * w
    return out


def kernel(
    zc, slabs, q_in, qt_in, k_in, v_in, kt_in, vt_in, list_in, count_in, out_ref,
    kv, qq, lst, cnt, bias, s_scr, p_scr, ps_scr, send, sstat, recv, rstat, coef,
    local_sem, ks, kr, qs, qr, qf, bs, rs, rr, ts, tr,
):
    rows, hd = q_in.shape
    half = rows // 2
    bits = zc.bit_length() - 1
    scale = 1.0 / math.sqrt(hd)
    factor = scale * math.log2(math.e)
    pb, kvi = lax.axis_index("pb"), lax.axis_index("kv")
    y, c, z, x = pb // 2, pb % 2, kvi // 2, kvi % 2
    inner = (z % 4 + 1) // 2 % 2
    to_x = (pb, kvi + 1 - 2 * x)
    to_y = (pb + 2 - 4 * y, kvi)
    to_c = (pb + 1 - 2 * c, kvi)

    def to_z(mask):
        return (pb, flip(z, mask, bits) * 2 + x)

    loads = []
    for n, (src, dst) in enumerate(
        [
            (k_in, kv.at[0, :, pl.ds(0, hd)]),
            (kt_in, kv.at[0, :, pl.ds(hd, hd)]),
            (v_in, kv.at[0, :, pl.ds(2 * hd, hd)]),
            (vt_in, kv.at[0, :, pl.ds(3 * hd, hd)]),
            (qt_in, qq.at[0, :, pl.ds(0, hd)]),
            (q_in, qq.at[0, :, pl.ds(hd, hd)]),
            (list_in, lst.at[0]),
            (count_in, cnt.at[0]),
        ]
    ):
        copy = pltpu.make_async_copy(src, dst, local_sem.at[n])
        copy.start()
        loads.append(copy)

    barrier = pltpu.get_barrier_semaphore()
    for dev in [to_x, to_y, to_c] + [to_z(m) for m in range(1, zc)]:
        pl.semaphore_signal(barrier, inc=1, device_id=dev, device_id_type=MESH)
    pl.semaphore_wait(barrier, 2 + zc)
    for copy in loads:
        copy.wait()

    def remote(src, dst, ssem, rsem, dev):
        return pltpu.make_async_remote_copy(
            src_ref=src, dst_ref=dst, send_sem=ssem, recv_sem=rsem,
            device_id=dev, device_id_type=MESH,
        )

    sent = []

    def piece(slot, h):
        return kv.at[slot, pl.ds(h * half, half)]

    def give(slot, h, dst, dev):
        copy = remote(piece(slot, h), piece(dst, h), ks.at[dst, h], kr.at[dst, h], dev)
        copy.start()
        sent.append(copy)

    def got(slot, h):
        remote(piece(slot, h), piece(slot, h), ks.at[slot, h], kr.at[slot, h], to_c).wait_recv()

    def chunk(m, h):
        return qq.at[m, pl.ds(h * half, half)]

    def ask(m, slot, h, sem, dev):
        return remote(chunk(m, h), chunk(slot, h), sem, qr.at[slot, h], dev)

    def got_chunk(m, h):
        ask(0, m, h, qs.at[m, h], to_c).wait_recv()

    def pass_on(m, h):
        @pl.when(inner == 1)
        def _():
            got_chunk(m, h)
            ask(m, 5 - m, h, qf.at[m - 2, h], to_z(1)).start()

    give(0, 1, 1, to_x)
    give(0, 0, 2, to_y)
    give(0, 0, 1, to_x)
    give(0, 1, 2, to_y)
    for m in [1 + 2 * inner, 2 - inner] + list(range(4, zc)):
        for h in range(2):
            copy = ask(0, m, h, qs.at[m, h], to_z(m))
            copy.start()
            sent.append(copy)
    give(0, 0, 4, to_c)
    give(0, 1, 4, to_c)
    tables = [
        remote(lst.at[0], lst.at[1], bs.at[0], bs.at[1], to_x),
        remote(cnt.at[0], cnt.at[1], bs.at[2], bs.at[3], to_x),
    ]
    for copy in tables:
        copy.start()

    def mask_rows(side):
        blocks = lst.shape[2]
        shard_blocks = rows // BLK
        slab_blocks = 4 * shard_blocks
        ids = lst[side]
        local = ids // (shard_blocks * slabs) * shard_blocks + ids % shard_blocks
        used = lax.broadcasted_iota(jnp.int32, ids.shape, 0) < cnt[side]
        row = lax.broadcasted_iota(jnp.int32, (slab_blocks, blocks), 0)
        on = jnp.zeros((slab_blocks, blocks), jnp.float32)
        for g in range(slab_blocks):
            hit = jnp.max(jnp.where((local == g) & used, 1.0, 0.0), axis=0, keepdims=True)
            on = jnp.where(row == g, hit, on)
        spread = jnp.where(
            lax.broadcasted_iota(jnp.int32, (slab_blocks, 4 * rows), 1) // BLK
            == lax.broadcasted_iota(jnp.int32, (slab_blocks, 4 * rows), 0),
            1.0, 0.0,
        )
        full = lax.dot_general(
            on, spread, (((0,), (0,)), ((), ())), preferred_element_type=jnp.float32
        )
        full = (full - 1.0) * 1e30
        for g in range(blocks):
            for p in range(4):
                bias[side, g, p] = full[g : g + 1, p * rows : (p + 1) * rows]

    def partial(mask, pieces):
        zt = flip(z, mask, bits)
        best = None
        at = 0
        spans = []
        for r, h in pieces:
            pbr = flip(pb, (r // 2) % 2 * 2 + r // 4, 2)
            lo, hi = (0, rows) if h is None else (h * half, h * half + half)
            s = lax.dot_general(
                qq[mask, :, hd:], kv[r, lo:hi, 0:hd], NT, preferred_element_type=jnp.float32
            )
            s = jnp.concatenate(
                [
                    s[g * half : (g + 1) * half]
                    + bias[r % 2, (zt * 2 + x) * 2 + g, pbr][:, lo:hi]
                    for g in range(2)
                ],
                axis=0,
            )
            s_scr[:, at : at + hi - lo] = s
            for g in range(0, hi - lo, hd):
                top = s[:, g : g + hd]
                best = top if best is None else jnp.maximum(best, top)
            spans.append((r, lo, hi, at))
            at += hi - lo
        peak = jnp.max(best, axis=1, keepdims=True)
        total = slope = both = tang = None
        for r, lo, hi, at in spans:
            p = jnp.exp2((s_scr[:, at : at + hi - lo] - peak) * factor)
            t = lax.dot_general(
                qq[mask], kv[r, lo:hi, 0 : 2 * hd], NT, preferred_element_type=jnp.float32
            )
            pt = p * t
            p_scr[:, at : at + hi - lo] = p.astype(jnp.bfloat16)
            ps_scr[:, at : at + hi - lo] = pt.astype(jnp.bfloat16)
            for g in range(0, hi - lo, hd):
                p2, pt2 = p[:, g : g + hd], pt[:, g : g + hd]
                total = p2 if total is None else total + p2
                slope = pt2 if slope is None else slope + pt2
        total = jnp.sum(total, axis=1, keepdims=True)
        slope = jnp.sum(slope, axis=1, keepdims=True)
        for r, lo, hi, at in spans:
            a = jnp.dot(
                p_scr[:, at : at + hi - lo], kv[r, lo:hi, 2 * hd :],
                preferred_element_type=jnp.float32,
            )
            b = jnp.dot(
                ps_scr[:, at : at + hi - lo], kv[r, lo:hi, 2 * hd : 3 * hd],
                preferred_element_type=jnp.float32,
            )
            both = a if both is None else both + a
            tang = b if tang is None else tang + b
        return peak, total, slope, both[:, :hd], tang * scale + both[:, hd:]

    def close(peak, total, slope, weighted, tang):
        mean = slope * scale / total
        centred = tang - mean * weighted
        lane = lax.broadcasted_iota(jnp.int32, (rows, hd), 1)
        stats = jnp.where(lane == 0, peak, jnp.where(lane == 1, total, mean))
        return weighted, centred, stats.T[0:8]

    def join(a, b):
        peak = jnp.maximum(a[0], b[0])
        fa, fb = jnp.exp2((a[0] - peak) * factor), jnp.exp2((b[0] - peak) * factor)
        return (peak,) + tuple(fa * m + fb * n for m, n in zip(a[1:], b[1:]))

    def result_copies(mask):
        dev = to_z(1 + inner) if isinstance(mask, int) and mask == 2 else to_z(mask)
        return (
            remote(send.at[mask], recv.at[mask], rs.at[mask], rr.at[mask], dev),
            remote(sstat.at[mask], rstat.at[mask], ts.at[mask], tr.at[mask], dev),
        )

    def hand_in(mask, weighted, centred, stats):
        send[mask, :, 0:hd] = weighted.astype(jnp.bfloat16)
        send[mask, :, hd:] = centred.astype(jnp.bfloat16)
        sstat[mask] = stats
        for copy in result_copies(mask):
            copy.start()

    def got_result(mask):
        for copy in result_copies(mask):
            copy.wait_recv()

    def got_queries(mask):
        for h in range(2):
            got_chunk(mask, h)

    most = tuple((r, None) for r in (0, 1, 2, 4, 5, 6))
    last = ((3, None), (7, None))
    whole = most + last

    mask_rows(0)
    pass_on(3, 0)
    got(2, 0)
    give(2, 0, 3, to_x)
    give(2, 0, 6, to_c)
    got(1, 1)
    give(1, 1, 3, to_y)
    give(1, 1, 5, to_c)
    pass_on(3, 1)
    pass_on(2, 0)
    got(1, 0)
    give(1, 0, 5, to_c)
    got(2, 1)
    give(2, 1, 6, to_c)
    pass_on(2, 1)
    for copy in tables:
        copy.wait_recv()
    mask_rows(1)

    @pl.when(inner == 0)
    def _():
        got_queries(2)

    for slot in (4, 5, 6):
        for h in range(2):
            got(slot, h)
    second = partial(2, most)
    for h in range(2):
        got(3, h)
        give(3, h, 7, to_c)

    @pl.when(inner == 0)
    def _():
        got_queries(3)

    for h in range(2):
        got(7, h)
    hand_in(2, *close(*join(second, partial(2, last))))
    third = partial(3, whole)

    @pl.when(inner == 0)
    def _():
        hand_in(3, *close(*third))

    got_queries(1)
    hand_in(1, *close(*partial(1, whole)))

    def step(mask, carry):
        got_queries(mask)
        hand_in(mask, *close(*partial(mask, whole)))
        return carry

    if zc > 4:
        lax.fori_loop(4, zc, step, 0)
    own = partial(0, whole)
    own_w, own_c, own_stats = close(*own)
    recv[0, :, 0:hd] = own_w.astype(jnp.bfloat16)
    recv[0, :, hd:] = own_c.astype(jnp.bfloat16)
    rstat[0] = own_stats
    coef[...] = jnp.zeros_like(coef)
    got_result(2)

    @pl.when(inner == 1)
    def _():
        coef[0:8, :] = rstat[2]
        cols = coef[...].T
        pk, tot, mean = cols[:, 0:1], cols[:, 1:2], cols[:, 2:3]
        w = recv[2, :, 0:hd].astype(jnp.float32)
        d = recv[2, :, hd:].astype(jnp.float32)
        both = join(third, (pk, tot, mean * tot / scale, w, d + mean * w))
        hand_in(3, *close(*both))
        recv[2] = jnp.zeros_like(recv[2])
        rstat[2] = jnp.concatenate([rstat[0, 0:1, :], jnp.zeros((7, rows), jnp.float32)], axis=0)
        coef[0:8, :] = jnp.zeros((8, rows), jnp.float32)

    for m in [1, 3] + list(range(4, zc)):
        got_result(m)

    peaks = [rstat[m, 0:1, :] for m in range(zc)]
    peak = functools.reduce(jnp.maximum, peaks)
    shares = [jnp.exp2((pk - peak) * factor) for pk in peaks]
    total = sum(a * rstat[m, 1:2, :] for m, a in enumerate(shares))
    mean = sum(a * rstat[m, 1:2, :] * rstat[m, 2:3, :] for m, a in enumerate(shares)) / total
    for m, a in enumerate(shares):
        a = a / total
        coef[2 * m : 2 * m + 1, :] = a
        coef[2 * m + 1 : 2 * m + 2, :] = a * (rstat[m, 2:3, :] - mean)
    columns = coef[...].T
    out = outt = 0.0
    for m in range(zc):
        w = recv[m, :, 0:hd].astype(jnp.float32)
        d = recv[m, :, hd:].astype(jnp.float32)
        a, g = columns[:, 2 * m : 2 * m + 1], columns[:, 2 * m + 1 : 2 * m + 2]
        out = out + a * w
        outt = outt + (a * d + g * w)
    out_ref[:, 0:hd] = out.astype(out_ref.dtype)
    out_ref[:, hd:] = outt.astype(out_ref.dtype)
    for copy in sent:
        copy.wait_send()

    @pl.when(inner == 1)
    def _():
        for m in (2, 3):
            for h in range(2):
                ask(m, 5 - m, h, qf.at[m - 2, h], to_z(1)).wait_send()

    for copy in tables:
        copy.wait_send()
    for m in range(1, zc):
        for copy in result_copies(m):
            copy.wait_send()


def shards(
    queries, query_tangent, keys, values, key_tangent, value_tangent, block_list, block_count
):
    rows, hd = keys.shape
    slabs, pbs = lax.axis_size("kv"), lax.axis_size("pb")
    zc = slabs // 2
    list_t = block_list[:, 0, :].T
    count_t = block_count.T
    blocks = list_t.shape[1]
    vmem = pl.BlockSpec(memory_space=pltpu.VMEM)
    hbm = pl.BlockSpec(memory_space=pl.ANY)
    dma = pltpu.SemaphoreType.DMA
    out = pl.pallas_call(
        functools.partial(kernel, zc, slabs),
        out_shape=jax.ShapeDtypeStruct((rows, 2 * hd), jnp.bfloat16),
        in_specs=[hbm] * 8,
        out_specs=vmem,
        scratch_shapes=[
            pltpu.VMEM((8, rows, 4 * hd), jnp.bfloat16),
            pltpu.VMEM((zc, rows, 2 * hd), jnp.bfloat16),
            pltpu.VMEM((2,) + list_t.shape, jnp.int32),
            pltpu.VMEM((2, 1, blocks), jnp.int32),
            pltpu.VMEM((2, blocks, pbs, 1, rows), jnp.float32),
            pltpu.VMEM((rows, 8 * rows), jnp.float32),
            pltpu.VMEM((rows, 8 * rows), jnp.bfloat16),
            pltpu.VMEM((rows, 8 * rows), jnp.bfloat16),
            pltpu.VMEM((zc, rows, 2 * hd), jnp.bfloat16),
            pltpu.VMEM((zc, 8, rows), jnp.float32),
            pltpu.VMEM((zc, rows, 2 * hd), jnp.bfloat16),
            pltpu.VMEM((zc, 8, rows), jnp.float32),
            pltpu.VMEM((128, rows), jnp.float32),
            dma((8,)),
            dma((8, 2)),
            dma((8, 2)),
            dma((zc, 2)),
            dma((zc, 2)),
            dma((2, 2)),
            dma((4,)),
            dma((zc,)),
            dma((zc,)),
            dma((zc,)),
            dma((zc,)),
        ],
        compiler_params=pltpu.CompilerParams(
            collective_id=0, has_side_effects=True, vmem_limit_bytes=62 * 1024 * 1024
        ),
    )(queries, query_tangent, keys, values, key_tangent, value_tangent, list_t, count_t)
    return out[:, :hd], out[:, hd:]


def solution(mesh):
    rows = P(("pb", "kv"), None)
    return jax.shard_map(
        shards,
        mesh=mesh,
        in_specs=(rows,) * 6 + (P("pb", "kv", None), P("pb", "kv")),
        out_specs=(rows, rows),
        check_vma=False,
    )
```

```python
import functools
import math

import jax
import jax.numpy as jnp
from jax import lax
from jax.experimental import pallas as pl
from jax.experimental.pallas import tpu as pltpu
from jax.sharding import PartitionSpec as P

BLK = 128
NT = (((1,), (1,)), ((), ()))
MESH = pl.DeviceIdType.MESH


def flip(a, b, bits):
    out = 0
    for k in range(bits):
        w = 1 << k
        out = out + (a // w + b // w) % 2 * w
    return out


def kernel(
    zc, slabs, q_in, qt_in, k_in, v_in, kt_in, vt_in, list_in, count_in, out_ref,
    kv, qq, lst, cnt, bias, s_scr, p_scr, ps_scr, send, sstat, recv, rstat, coef,
    local_sem, ks, kr, qs, qr, qf, bs, rs, rr, ts, tr,
):
    rows, hd = q_in.shape
    half = rows // 2
    bits = zc.bit_length() - 1
    scale = 1.0 / math.sqrt(hd)
    factor = scale * math.log2(math.e)
    pb, kvi = lax.axis_index("pb"), lax.axis_index("kv")
    y, c, z, x = pb // 2, pb % 2, kvi // 2, kvi % 2
    inner = (z % 4 + 1) // 2 % 2
    to_x = (pb, kvi + 1 - 2 * x)
    to_y = (pb + 2 - 4 * y, kvi)
    to_c = (pb + 1 - 2 * c, kvi)

    def to_z(mask):
        return (pb, flip(z, mask, bits) * 2 + x)

    barrier = pltpu.get_barrier_semaphore()
    for dev in [to_x, to_y, to_c] + [to_z(m) for m in range(1, zc)]:
        pl.semaphore_signal(barrier, inc=1, device_id=dev, device_id_type=MESH)
    for n, (src, dst) in enumerate(
        [
            (k_in, kv.at[0, :, pl.ds(0, hd)]),
            (kt_in, kv.at[0, :, pl.ds(hd, hd)]),
            (v_in, kv.at[0, :, pl.ds(2 * hd, hd)]),
            (vt_in, kv.at[0, :, pl.ds(3 * hd, hd)]),
            (qt_in, qq.at[0, :, pl.ds(0, hd)]),
            (q_in, qq.at[0, :, pl.ds(hd, hd)]),
            (list_in, lst.at[0]),
            (count_in, cnt.at[0]),
        ]
    ):
        pltpu.make_async_copy(src, dst, local_sem.at[max(n // 4, n - 4)]).start()

    pl.semaphore_wait(barrier, 2 + zc)
    for n, ref in enumerate((kv.at[0], qq.at[0], lst.at[0], cnt.at[0])):
        pltpu.make_async_copy(ref, ref, local_sem.at[n]).wait()

    def remote(src, dst, ssem, rsem, dev):
        return pltpu.make_async_remote_copy(
            src_ref=src, dst_ref=dst, send_sem=ssem, recv_sem=rsem,
            device_id=dev, device_id_type=MESH,
        )

    def piece(slot, h):
        return kv.at[slot, pl.ds(h * half, half)]

    def give(slot, h, dst, dev):
        copy = remote(piece(slot, h), piece(dst, h), ks.at[0], kr.at[dst, h], dev)
        copy.start()

    def got(slot, h):
        remote(piece(slot, h), piece(slot, h), ks.at[0], kr.at[slot, h], to_c).wait_recv()

    def chunk(m, h):
        return qq.at[m, pl.ds(h * half, half)]

    def ask(m, slot, h, sem, dev):
        return remote(chunk(m, h), chunk(slot, h), sem, qr.at[slot, h], dev)

    def got_chunk(m, h):
        ask(0, m, h, qs.at[0], to_c).wait_recv()

    def pass_on(m, h):
        @pl.when(inner == 1)
        def _():
            got_chunk(m, h)
            ask(m, 5 - m, h, qf.at[0], to_z(1)).start()

    give(0, 1, 1, to_x)
    give(0, 0, 2, to_y)
    give(0, 0, 1, to_x)
    give(0, 1, 2, to_y)
    for m in [1 + 2 * inner, 2 - inner] + list(range(4, zc)):
        for h in range(2):
            copy = ask(0, m, h, qs.at[0], to_z(m))
            copy.start()
    give(0, 0, 4, to_c)
    give(0, 1, 4, to_c)
    tables = [
        remote(lst.at[0], lst.at[1], bs.at[0], bs.at[1], to_x),
        remote(cnt.at[0], cnt.at[1], bs.at[2], bs.at[3], to_x),
    ]
    for copy in tables:
        copy.start()

    def mask_rows(side):
        blocks = lst.shape[2]
        shard_blocks = rows // BLK
        slab_blocks = 4 * shard_blocks
        ids = lst[side]
        local = ids // (shard_blocks * slabs) * shard_blocks + ids % shard_blocks
        used = lax.broadcasted_iota(jnp.int32, ids.shape, 0) < cnt[side]
        row = lax.broadcasted_iota(jnp.int32, (slab_blocks, blocks), 0)
        on = jnp.zeros((slab_blocks, blocks), jnp.float32)
        for g in range(slab_blocks):
            hit = jnp.max(jnp.where((local == g) & used, 1.0, 0.0), axis=0, keepdims=True)
            on = jnp.where(row == g, hit, on)
        spread = jnp.where(
            lax.broadcasted_iota(jnp.int32, (slab_blocks, 4 * rows), 1) // BLK
            == lax.broadcasted_iota(jnp.int32, (slab_blocks, 4 * rows), 0),
            1.0, 0.0,
        )
        full = lax.dot_general(
            on, spread, (((0,), (0,)), ((), ())), preferred_element_type=jnp.float32
        )
        full = (full - 1.0) * 1e30
        for g in range(blocks):
            for p in range(4):
                bias[side, g, p] = full[g : g + 1, p * rows : (p + 1) * rows]

    def partial(mask, pieces):
        zt = flip(z, mask, bits)
        best = None
        at = 0
        spans = []
        for r, h in pieces:
            pbr = flip(pb, (r // 2) % 2 * 2 + r // 4, 2)
            lo, hi = (0, rows) if h is None else (h * half, h * half + half)
            s = lax.dot_general(
                qq[mask, :, hd:], kv[r, lo:hi, 0:hd], NT, preferred_element_type=jnp.float32
            )
            s = jnp.concatenate(
                [
                    s[g * half : (g + 1) * half]
                    + bias[r % 2, (zt * 2 + x) * 2 + g, pbr][:, lo:hi]
                    for g in range(2)
                ],
                axis=0,
            )
            s_scr[:, at : at + hi - lo] = s
            for g in range(0, hi - lo, hd):
                top = s[:, g : g + hd]
                best = top if best is None else jnp.maximum(best, top)
            spans.append((r, lo, hi, at))
            at += hi - lo
        peak = jnp.max(best, axis=1, keepdims=True)
        total = slope = both = tang = None
        for r, lo, hi, at in spans:
            p = jnp.exp2((s_scr[:, at : at + hi - lo] - peak) * factor)
            t = lax.dot_general(
                qq[mask], kv[r, lo:hi, 0 : 2 * hd], NT, preferred_element_type=jnp.float32
            )
            pt = p * t
            p_scr[:, at : at + hi - lo] = p.astype(jnp.bfloat16)
            ps_scr[:, at : at + hi - lo] = pt.astype(jnp.bfloat16)
            for g in range(0, hi - lo, hd):
                p2, pt2 = p[:, g : g + hd], pt[:, g : g + hd]
                total = p2 if total is None else total + p2
                slope = pt2 if slope is None else slope + pt2
        total = jnp.sum(total, axis=1, keepdims=True)
        slope = jnp.sum(slope, axis=1, keepdims=True)
        for r, lo, hi, at in spans:
            a = jnp.dot(
                p_scr[:, at : at + hi - lo], kv[r, lo:hi, 2 * hd :],
                preferred_element_type=jnp.float32,
            )
            b = jnp.dot(
                ps_scr[:, at : at + hi - lo], kv[r, lo:hi, 2 * hd : 3 * hd],
                preferred_element_type=jnp.float32,
            )
            both = a if both is None else both + a
            tang = b if tang is None else tang + b
        return peak, total, slope, both[:, :hd], tang * scale + both[:, hd:]

    def close(peak, total, slope, weighted, tang):
        mean = slope * scale / total
        centred = tang - mean * weighted
        lane = lax.broadcasted_iota(jnp.int32, (rows, hd), 1)
        stats = jnp.where(lane == 0, peak, jnp.where(lane == 1, total, mean))
        return weighted, centred, stats.T[0:8]

    def join(a, b):
        peak = jnp.maximum(a[0], b[0])
        fa, fb = jnp.exp2((a[0] - peak) * factor), jnp.exp2((b[0] - peak) * factor)
        return (peak,) + tuple(fa * m + fb * n for m, n in zip(a[1:], b[1:]))

    def result_copies(mask):
        dev = to_z(1 + inner) if isinstance(mask, int) and mask == 2 else to_z(mask)
        return (
            remote(send.at[mask], recv.at[mask], rs.at[0], rr.at[mask], dev),
            remote(sstat.at[mask], rstat.at[mask], ts.at[0], tr.at[mask], dev),
        )

    def hand_in(mask, weighted, centred, stats):
        send[mask, :, 0:hd] = weighted.astype(jnp.bfloat16)
        send[mask, :, hd:] = centred.astype(jnp.bfloat16)
        sstat[mask] = stats
        for copy in result_copies(mask):
            copy.start()

    def got_result(mask):
        for copy in result_copies(mask):
            copy.wait_recv()

    def got_queries(mask):
        for h in range(2):
            got_chunk(mask, h)

    most = tuple((r, None) for r in (0, 1, 2, 4, 5, 6))
    last = ((3, None), (7, None))
    whole = most + last

    mask_rows(0)
    pass_on(3, 0)
    got(2, 0)
    give(2, 0, 3, to_x)
    give(2, 0, 6, to_c)
    got(1, 1)
    give(1, 1, 3, to_y)
    give(1, 1, 5, to_c)
    pass_on(3, 1)
    pass_on(2, 0)
    got(1, 0)
    give(1, 0, 5, to_c)
    got(2, 1)
    give(2, 1, 6, to_c)
    pass_on(2, 1)
    for copy in tables:
        copy.wait_recv()
    mask_rows(1)

    @pl.when(inner == 0)
    def _():
        got_queries(2)

    for slot in (4, 5, 6):
        for h in range(2):
            got(slot, h)
    second = partial(2, most)
    for h in range(2):
        got(3, h)
        give(3, h, 7, to_c)

    @pl.when(inner == 0)
    def _():
        got_queries(3)

    for h in range(2):
        got(7, h)
    hand_in(2, *close(*join(second, partial(2, last))))
    third = partial(3, whole)

    @pl.when(inner == 0)
    def _():
        hand_in(3, *close(*third))

    got_queries(1)
    hand_in(1, *close(*partial(1, whole)))

    def step(mask, carry):
        got_queries(mask)
        hand_in(mask, *close(*partial(mask, whole)))
        return carry

    if zc > 4:
        lax.fori_loop(4, zc, step, 0)
    own = partial(0, whole)
    own_w, own_c, own_stats = close(*own)
    recv[0, :, 0:hd] = own_w.astype(jnp.bfloat16)
    recv[0, :, hd:] = own_c.astype(jnp.bfloat16)
    rstat[0] = own_stats
    coef[...] = jnp.zeros_like(coef)
    got_result(2)

    @pl.when(inner == 1)
    def _():
        coef[0:8, :] = rstat[2]
        cols = coef[...].T
        pk, tot, mean = cols[:, 0:1], cols[:, 1:2], cols[:, 2:3]
        w = recv[2, :, 0:hd].astype(jnp.float32)
        d = recv[2, :, hd:].astype(jnp.float32)
        both = join(third, (pk, tot, mean * tot / scale, w, d + mean * w))
        hand_in(3, *close(*both))
        recv[2] = jnp.zeros_like(recv[2])
        rstat[2] = jnp.concatenate([rstat[0, 0:1, :], jnp.zeros((7, rows), jnp.float32)], axis=0)
        coef[0:8, :] = jnp.zeros((8, rows), jnp.float32)

    for m in [1, 3] + list(range(4, zc)):
        got_result(m)

    peaks = [rstat[m, 0:1, :] for m in range(zc)]
    peak = functools.reduce(jnp.maximum, peaks)
    shares = [jnp.exp2((pk - peak) * factor) for pk in peaks]
    total = sum(a * rstat[m, 1:2, :] for m, a in enumerate(shares))
    mean = sum(a * rstat[m, 1:2, :] * rstat[m, 2:3, :] for m, a in enumerate(shares)) / total
    for m, a in enumerate(shares):
        a = a / total
        coef[2 * m : 2 * m + 1, :] = a
        coef[2 * m + 1 : 2 * m + 2, :] = a * (rstat[m, 2:3, :] - mean)
    columns = coef[...].T
    out = outt = 0.0
    for m in range(zc):
        w = recv[m, :, 0:hd].astype(jnp.float32)
        d = recv[m, :, hd:].astype(jnp.float32)
        a, g = columns[:, 2 * m : 2 * m + 1], columns[:, 2 * m + 1 : 2 * m + 2]
        out = out + a * w
        outt = outt + (a * d + g * w)
    out_ref[:, 0:hd] = out.astype(out_ref.dtype)
    out_ref[:, hd:] = outt.astype(out_ref.dtype)
    def all_sent(ref, sem):
        remote(ref, ref, sem, sem, to_c).wait_send()

    all_sent(kv.at[pl.ds(0, 7)], ks.at[0])
    all_sent(qq.at[pl.ds(0, 2 + max(zc - 4, 0))], qs.at[0])

    @pl.when(inner == 1)
    def _():
        all_sent(qq.at[pl.ds(0, 2)], qf.at[0])

    for copy in tables:
        copy.wait_send()
    all_sent(send.at[pl.ds(1, zc - 1)], rs.at[0])
    all_sent(sstat.at[pl.ds(1, zc - 1)], ts.at[0])


def shards(
    queries, query_tangent, keys, values, key_tangent, value_tangent, block_list, block_count
):
    rows, hd = keys.shape
    slabs, pbs = lax.axis_size("kv"), lax.axis_size("pb")
    zc = slabs // 2
    list_t = block_list[:, 0, :].T
    count_t = block_count.T
    blocks = list_t.shape[1]
    vmem = pl.BlockSpec(memory_space=pltpu.VMEM)
    hbm = pl.BlockSpec(memory_space=pl.ANY)
    dma = pltpu.SemaphoreType.DMA
    out = pl.pallas_call(
        functools.partial(kernel, zc, slabs),
        out_shape=jax.ShapeDtypeStruct((rows, 2 * hd), jnp.bfloat16),
        in_specs=[hbm] * 8,
        out_specs=vmem,
        scratch_shapes=[
            pltpu.VMEM((8, rows, 4 * hd), jnp.bfloat16),
            pltpu.VMEM((zc, rows, 2 * hd), jnp.bfloat16),
            pltpu.VMEM((2,) + list_t.shape, jnp.int32),
            pltpu.VMEM((2, 1, blocks), jnp.int32),
            pltpu.VMEM((2, blocks, pbs, 1, rows), jnp.float32),
            pltpu.VMEM((rows, 8 * rows), jnp.float32),
            pltpu.VMEM((rows, 8 * rows), jnp.bfloat16),
            pltpu.VMEM((rows, 8 * rows), jnp.bfloat16),
            pltpu.VMEM((zc, rows, 2 * hd), jnp.bfloat16),
            pltpu.VMEM((zc, 8, rows), jnp.float32),
            pltpu.VMEM((zc, rows, 2 * hd), jnp.bfloat16),
            pltpu.VMEM((zc, 8, rows), jnp.float32),
            pltpu.VMEM((128, rows), jnp.float32),
            dma((4,)),
            dma((1,)),
            dma((8, 2)),
            dma((1,)),
            dma((zc, 2)),
            dma((1,)),
            dma((4,)),
            dma((1,)),
            dma((zc,)),
            dma((1,)),
            dma((zc,)),
        ],
        compiler_params=pltpu.CompilerParams(
            collective_id=0, has_side_effects=True, vmem_limit_bytes=20 * 1024 * 1024
        ),
    )(*[pltpu.with_memory_space_constraint(a, pltpu.HBM) for a in (queries, query_tangent, keys, values, key_tangent, value_tangent, list_t, count_t)])
    return out[:, :hd], out[:, hd:]


def solution(mesh):
    rows = P(("pb", "kv"), None)
    return jax.shard_map(
        shards,
        mesh=mesh,
        in_specs=(rows,) * 6 + (P("pb", "kv", None), P("pb", "kv")),
        out_specs=(rows, rows),
        check_vma=False,
    )
```

```python
import functools
import math

import jax
import jax.numpy as jnp
from jax import lax
from jax.experimental import pallas as pl
from jax.experimental.pallas import tpu as pltpu
from jax.sharding import PartitionSpec as P

BLK = 128
NT = (((1,), (1,)), ((), ()))
MESH = pl.DeviceIdType.MESH


def flip(a, b, bits):
    out = 0
    for k in range(bits):
        w = 1 << k
        out = out + (a // w + b // w) % 2 * w
    return out


def kernel(
    zc, slabs, q_in, qt_in, k_in, v_in, kt_in, vt_in, list_in, count_in, out_ref,
    kv, qq, lst, cnt, bias, s_scr, p_scr, ps_scr, send, sstat, recv, rstat, coef,
    local_sem, ks, kr, qs, qr, qf, bs, rs, rr, ts, tr,
):
    rows, hd = q_in.shape
    half = rows // 2
    bits = zc.bit_length() - 1
    scale = 1.0 / math.sqrt(hd)
    factor = scale * math.log2(math.e)
    pb, kvi = lax.axis_index("pb"), lax.axis_index("kv")
    y, c, z, x = pb // 2, pb % 2, kvi // 2, kvi % 2
    inner = (z % 4 + 1) // 2 % 2
    to_x = (pb, kvi + 1 - 2 * x)
    to_y = (pb + 2 - 4 * y, kvi)
    to_c = (pb + 1 - 2 * c, kvi)

    def to_z(mask):
        return (pb, flip(z, mask, bits) * 2 + x)

    barrier = pltpu.get_barrier_semaphore()
    for dev in [to_x, to_y, to_c] + [to_z(m) for m in range(1, zc)]:
        pl.semaphore_signal(barrier, inc=1, device_id=dev, device_id_type=MESH)
    for n, (src, dst) in enumerate(
        [
            (k_in, kv.at[0, :, pl.ds(0, hd)]),
            (kt_in, kv.at[0, :, pl.ds(hd, hd)]),
            (v_in, kv.at[0, :, pl.ds(2 * hd, hd)]),
            (vt_in, kv.at[0, :, pl.ds(3 * hd, hd)]),
            (qt_in, qq.at[0, :, pl.ds(0, hd)]),
            (q_in, qq.at[0, :, pl.ds(hd, hd)]),
            (list_in, lst.at[0]),
            (count_in, cnt.at[0]),
        ]
    ):
        pltpu.make_async_copy(src, dst, local_sem.at[max(n // 4, n - 4)]).start()

    pl.semaphore_wait(barrier, 2 + zc)
    for n, ref in enumerate((kv.at[0], qq.at[0], lst.at[0], cnt.at[0])):
        pltpu.make_async_copy(ref, ref, local_sem.at[n]).wait()

    def remote(src, dst, ssem, rsem, dev):
        return pltpu.make_async_remote_copy(
            src_ref=src, dst_ref=dst, send_sem=ssem, recv_sem=rsem,
            device_id=dev, device_id_type=MESH,
        )

    def piece(slot, h):
        return kv.at[slot, pl.ds(h * half, half)]

    def give(slot, h, dst, dev):
        copy = remote(piece(slot, h), piece(dst, h), ks.at[0], kr.at[dst, h], dev)
        copy.start()

    def got(slot, h):
        remote(piece(slot, h), piece(slot, h), ks.at[0], kr.at[slot, h], to_c).wait_recv()

    def chunk(m, h):
        return qq.at[m, pl.ds(h * half, half)]

    def ask(m, slot, h, sem, dev):
        return remote(chunk(m, h), chunk(slot, h), sem, qr.at[slot, h], dev)

    def got_chunk(m, h):
        ask(0, m, h, qs.at[0], to_c).wait_recv()

    def pass_on(m, h):
        @pl.when(inner == 1)
        def _():
            got_chunk(m, h)
            ask(m, 5 - m, h, qf.at[0], to_z(1)).start()

    give(0, 1, 1, to_x)
    give(0, 0, 2, to_y)
    give(0, 0, 1, to_x)
    give(0, 1, 2, to_y)
    for m in [1 + 2 * inner, 2 - inner] + list(range(4, zc)):
        for h in range(2):
            copy = ask(0, m, h, qs.at[0], to_z(m))
            copy.start()
    give(0, 0, 4, to_c)
    give(0, 1, 4, to_c)
    tables = [
        remote(lst.at[0], lst.at[1], bs.at[0], bs.at[1], to_x),
        remote(cnt.at[0], cnt.at[1], bs.at[2], bs.at[3], to_x),
    ]
    for copy in tables:
        copy.start()

    def mask_rows(side):
        blocks = lst.shape[2]
        shard_blocks = rows // BLK
        slab_blocks = 4 * shard_blocks
        ids = lst[side]
        local = ids // (shard_blocks * slabs) * shard_blocks + ids % shard_blocks
        used = lax.broadcasted_iota(jnp.int32, ids.shape, 0) < cnt[side]
        row = lax.broadcasted_iota(jnp.int32, (slab_blocks, blocks), 0)
        on = jnp.zeros((slab_blocks, blocks), jnp.float32)
        for g in range(slab_blocks):
            hit = jnp.max(jnp.where((local == g) & used, 1.0, 0.0), axis=0, keepdims=True)
            on = jnp.where(row == g, hit, on)
        spread = jnp.where(
            lax.broadcasted_iota(jnp.int32, (slab_blocks, 4 * rows), 1) // BLK
            == lax.broadcasted_iota(jnp.int32, (slab_blocks, 4 * rows), 0),
            1.0, 0.0,
        )
        full = lax.dot_general(
            on, spread, (((0,), (0,)), ((), ())), preferred_element_type=jnp.float32
        )
        full = (full - 1.0) * 1e30
        for g in range(blocks):
            for p in range(4):
                bias[side, g, p] = full[g : g + 1, p * rows : (p + 1) * rows]

    def partial(mask, pieces):
        zt = flip(z, mask, bits)
        best = None
        at = 0
        spans = []
        for r, h in pieces:
            pbr = flip(pb, (r // 2) % 2 * 2 + r // 4, 2)
            lo, hi = (0, rows) if h is None else (h * half, h * half + half)
            s = lax.dot_general(
                qq[mask, :, hd:], kv[r, lo:hi, 0:hd], NT, preferred_element_type=jnp.float32
            )
            s = jnp.concatenate(
                [
                    s[g * half : (g + 1) * half]
                    + bias[r % 2, (zt * 2 + x) * 2 + g, pbr][:, lo:hi]
                    for g in range(2)
                ],
                axis=0,
            )
            s_scr[:, at : at + hi - lo] = s
            for g in range(0, hi - lo, hd):
                top = s[:, g : g + hd]
                best = top if best is None else jnp.maximum(best, top)
            spans.append((r, lo, hi, at))
            at += hi - lo
        peak = jnp.max(best, axis=1, keepdims=True)
        total = slope = both = tang = None
        for r, lo, hi, at in spans:
            p = jnp.exp2((s_scr[:, at : at + hi - lo] - peak) * factor)
            t = lax.dot_general(
                qq[mask], kv[r, lo:hi, 0 : 2 * hd], NT, preferred_element_type=jnp.float32
            )
            pt = p * t
            p_scr[:, at : at + hi - lo] = p.astype(jnp.bfloat16)
            ps_scr[:, at : at + hi - lo] = pt.astype(jnp.bfloat16)
            for g in range(0, hi - lo, hd):
                p2, pt2 = p[:, g : g + hd], pt[:, g : g + hd]
                total = p2 if total is None else total + p2
                slope = pt2 if slope is None else slope + pt2
        total = jnp.sum(total, axis=1, keepdims=True)
        slope = jnp.sum(slope, axis=1, keepdims=True)
        for r, lo, hi, at in spans:
            a = jnp.dot(
                p_scr[:, at : at + hi - lo], kv[r, lo:hi, 2 * hd :],
                preferred_element_type=jnp.float32,
            )
            b = jnp.dot(
                ps_scr[:, at : at + hi - lo], kv[r, lo:hi, 2 * hd : 3 * hd],
                preferred_element_type=jnp.float32,
            )
            both = a if both is None else both + a
            tang = b if tang is None else tang + b
        return peak, total, slope, both[:, :hd], tang * scale + both[:, hd:]

    def close(peak, total, slope, weighted, tang):
        mean = slope * scale / total
        centred = tang - mean * weighted
        lane = lax.broadcasted_iota(jnp.int32, (rows, hd), 1)
        stats = jnp.where(lane == 0, peak, jnp.where(lane == 1, total, mean))
        flat = stats.T[0:4]
        return weighted, centred, jnp.concatenate([flat[:, :half], flat[:, half:]], axis=0)

    def join(a, b):
        peak = jnp.maximum(a[0], b[0])
        fa, fb = jnp.exp2((a[0] - peak) * factor), jnp.exp2((b[0] - peak) * factor)
        return (peak,) + tuple(fa * m + fb * n for m, n in zip(a[1:], b[1:]))

    def result_copies(mask):
        dev = to_z(1 + inner) if isinstance(mask, int) and mask == 2 else to_z(mask)
        return (
            remote(send.at[mask], recv.at[mask], rs.at[0], rr.at[mask], dev),
            remote(sstat.at[mask], rstat.at[mask], ts.at[0], tr.at[mask], dev),
        )

    def hand_in(mask, weighted, centred, stats):
        send[mask, :, 0:hd] = weighted.astype(jnp.bfloat16)
        send[mask, :, hd:] = centred.astype(jnp.bfloat16)
        sstat[mask] = stats
        for copy in result_copies(mask):
            copy.start()

    def got_result(mask):
        for copy in result_copies(mask):
            copy.wait_recv()

    def got_queries(mask):
        for h in range(2):
            got_chunk(mask, h)

    most = tuple((r, None) for r in (0, 1, 2, 4, 5, 6))
    last = ((3, None), (7, None))
    whole = most + last

    mask_rows(0)
    pass_on(3, 0)
    got(2, 0)
    give(2, 0, 3, to_x)
    give(2, 0, 6, to_c)
    got(1, 1)
    give(1, 1, 3, to_y)
    give(1, 1, 5, to_c)
    pass_on(3, 1)
    pass_on(2, 0)
    got(1, 0)
    give(1, 0, 5, to_c)
    got(2, 1)
    give(2, 1, 6, to_c)
    pass_on(2, 1)
    for copy in tables:
        copy.wait_recv()
    mask_rows(1)

    @pl.when(inner == 0)
    def _():
        got_queries(2)

    for slot in (4, 5, 6):
        for h in range(2):
            got(slot, h)
    second = partial(2, most)
    for h in range(2):
        got(3, h)
        give(3, h, 7, to_c)

    @pl.when(inner == 0)
    def _():
        got_queries(3)

    for h in range(2):
        got(7, h)
    hand_in(2, *close(*join(second, partial(2, last))))
    third = partial(3, whole)

    @pl.when(inner == 0)
    def _():
        hand_in(3, *close(*third))

    got_queries(1)
    hand_in(1, *close(*partial(1, whole)))

    def step(mask, carry):
        got_queries(mask)
        hand_in(mask, *close(*partial(mask, whole)))
        return carry

    if zc > 4:
        lax.fori_loop(4, zc, step, 0)
    own = partial(0, whole)
    own_w, own_c, own_stats = close(*own)
    recv[0, :, 0:hd] = own_w.astype(jnp.bfloat16)
    recv[0, :, hd:] = own_c.astype(jnp.bfloat16)
    rstat[0] = own_stats
    coef[...] = jnp.zeros_like(coef)
    got_result(2)

    @pl.when(inner == 1)
    def _():
        coef[0:4, :half], coef[0:4, half:] = rstat[2, 0:4], rstat[2, 4:8]
        cols = coef[...].T
        pk, tot, mean = cols[:, 0:1], cols[:, 1:2], cols[:, 2:3]
        w = recv[2, :, 0:hd].astype(jnp.float32)
        d = recv[2, :, hd:].astype(jnp.float32)
        both = join(third, (pk, tot, mean * tot / scale, w, d + mean * w))
        hand_in(3, *close(*both))
        recv[2] = jnp.zeros_like(recv[2])
        lane = lax.broadcasted_iota(jnp.int32, rstat.shape[1:], 0)
        rstat[2] = jnp.where(lane % 4 == 0, rstat[0], 0.0)
        coef[0:8, :] = jnp.zeros((8, rows), jnp.float32)

    for m in [1, 3] + list(range(4, zc)):
        got_result(m)

    def stat(m, n):
        return jnp.concatenate([rstat[m, n : n + 1], rstat[m, n + 4 : n + 5]], axis=1)

    peaks = [stat(m, 0) for m in range(zc)]
    peak = functools.reduce(jnp.maximum, peaks)
    shares = [jnp.exp2((pk - peak) * factor) for pk in peaks]
    total = sum(a * stat(m, 1) for m, a in enumerate(shares))
    mean = sum(a * stat(m, 1) * stat(m, 2) for m, a in enumerate(shares)) / total
    for m, a in enumerate(shares):
        a = a / total
        coef[2 * m : 2 * m + 1, :] = a
        coef[2 * m + 1 : 2 * m + 2, :] = a * (stat(m, 2) - mean)
    columns = coef[...].T
    out = outt = 0.0
    for m in range(zc):
        w = recv[m, :, 0:hd].astype(jnp.float32)
        d = recv[m, :, hd:].astype(jnp.float32)
        a, g = columns[:, 2 * m : 2 * m + 1], columns[:, 2 * m + 1 : 2 * m + 2]
        out = out + a * w
        outt = outt + (a * d + g * w)
    out_ref[:, 0:hd] = out.astype(out_ref.dtype)
    out_ref[:, hd:] = outt.astype(out_ref.dtype)
    def all_sent(ref, sem):
        remote(ref, ref, sem, sem, to_c).wait_send()

    all_sent(kv.at[pl.ds(0, 7)], ks.at[0])
    all_sent(qq.at[pl.ds(0, 2 + max(zc - 4, 0))], qs.at[0])

    @pl.when(inner == 1)
    def _():
        all_sent(qq.at[pl.ds(0, 2)], qf.at[0])

    for copy in tables:
        copy.wait_send()
    all_sent(send.at[pl.ds(1, zc - 1)], rs.at[0])
    all_sent(sstat.at[pl.ds(1, zc - 1)], ts.at[0])


def shards(
    queries, query_tangent, keys, values, key_tangent, value_tangent, block_list, block_count
):
    rows, hd = keys.shape
    slabs, pbs = lax.axis_size("kv"), lax.axis_size("pb")
    zc = slabs // 2
    list_t = block_list[:, 0, :].T
    count_t = block_count.T
    blocks = list_t.shape[1]
    vmem = pl.BlockSpec(memory_space=pltpu.VMEM)
    hbm = pl.BlockSpec(memory_space=pl.ANY)
    dma = pltpu.SemaphoreType.DMA
    out = pl.pallas_call(
        functools.partial(kernel, zc, slabs),
        out_shape=jax.ShapeDtypeStruct((rows, 2 * hd), jnp.bfloat16),
        in_specs=[hbm] * 8,
        out_specs=vmem,
        scratch_shapes=[
            pltpu.VMEM((8, rows, 4 * hd), jnp.bfloat16),
            pltpu.VMEM((zc, rows, 2 * hd), jnp.bfloat16),
            pltpu.VMEM((2,) + list_t.shape, jnp.int32),
            pltpu.VMEM((2, 1, blocks), jnp.int32),
            pltpu.VMEM((2, blocks, pbs, 1, rows), jnp.float32),
            pltpu.VMEM((rows, 8 * rows), jnp.float32),
            pltpu.VMEM((rows, 8 * rows), jnp.bfloat16),
            pltpu.VMEM((rows, 8 * rows), jnp.bfloat16),
            pltpu.VMEM((zc, rows, 2 * hd), jnp.bfloat16),
            pltpu.VMEM((zc, 8, rows // 2), jnp.float32),
            pltpu.VMEM((zc, rows, 2 * hd), jnp.bfloat16),
            pltpu.VMEM((zc, 8, rows // 2), jnp.float32),
            pltpu.VMEM((128, rows), jnp.float32),
            dma((4,)),
            dma((1,)),
            dma((8, 2)),
            dma((1,)),
            dma((zc, 2)),
            dma((1,)),
            dma((4,)),
            dma((1,)),
            dma((zc,)),
            dma((1,)),
            dma((zc,)),
        ],
        compiler_params=pltpu.CompilerParams(
            collective_id=0, has_side_effects=True, vmem_limit_bytes=20 * 1024 * 1024
        ),
    )(*[pltpu.with_memory_space_constraint(a, pltpu.HBM) for a in (queries, query_tangent, keys, values, key_tangent, value_tangent, list_t, count_t)])
    return out[:, :hd], out[:, hd:]


def solution(mesh):
    rows = P(("pb", "kv"), None)
    return jax.shard_map(
        shards,
        mesh=mesh,
        in_specs=(rows,) * 6 + (P("pb", "kv", None), P("pb", "kv")),
        out_specs=(rows, rows),
        check_vma=False,
    )
```

```python
import functools
import math

import jax
import jax.numpy as jnp
from jax import lax
from jax.experimental import pallas as pl
from jax.experimental.pallas import tpu as pltpu
from jax.sharding import PartitionSpec as P

BLK = 128
NT = (((1,), (1,)), ((), ()))
MESH = pl.DeviceIdType.MESH


def flip(a, b, bits):
    out = 0
    for k in range(bits):
        w = 1 << k
        out = out + (a // w + b // w) % 2 * w
    return out


def kernel(
    zc, slabs, q_in, qt_in, k_in, v_in, kt_in, vt_in, list_in, count_in, out_ref,
    kv, qq, lst, cnt, bias, s_scr, p_scr, ps_scr, send, sstat, recv, rstat, coef,
    local_sem, ks, kr, qs, qr, qf, bs, rs, rr, ts, tr,
):
    rows, hd = q_in.shape
    half = rows // 2
    bits = zc.bit_length() - 1
    scale = 1.0 / math.sqrt(hd)
    factor = scale * math.log2(math.e)
    pb, kvi = lax.axis_index("pb"), lax.axis_index("kv")
    y, c, z, x = pb // 2, pb % 2, kvi // 2, kvi % 2
    inner = (z % 4 + 1) // 2 % 2
    to_x = (pb, kvi + 1 - 2 * x)
    to_y = (pb + 2 - 4 * y, kvi)
    to_c = (pb + 1 - 2 * c, kvi)

    def to_z(mask):
        return (pb, flip(z, mask, bits) * 2 + x)

    barrier = pltpu.get_barrier_semaphore()
    for dev in [to_x, to_y, to_c] + [to_z(m) for m in range(1, zc)]:
        pl.semaphore_signal(barrier, inc=1, device_id=dev, device_id_type=MESH)
    for n, (src, dst) in enumerate(
        [
            (k_in, kv.at[0, :, pl.ds(0, hd)]),
            (kt_in, kv.at[0, :, pl.ds(hd, hd)]),
            (v_in, kv.at[0, :, pl.ds(2 * hd, hd)]),
            (vt_in, kv.at[0, :, pl.ds(3 * hd, hd)]),
            (qt_in, qq.at[0, :, pl.ds(0, hd)]),
            (q_in, qq.at[0, :, pl.ds(hd, hd)]),
            (list_in, lst.at[0]),
            (count_in, cnt.at[0]),
        ]
    ):
        pltpu.make_async_copy(src, dst, local_sem.at[max(n // 4, n - 4)]).start()

    pl.semaphore_wait(barrier, 2 + zc)
    for n, ref in enumerate((kv.at[0], qq.at[0], lst.at[0], cnt.at[0])):
        pltpu.make_async_copy(ref, ref, local_sem.at[n]).wait()

    def remote(src, dst, ssem, rsem, dev):
        return pltpu.make_async_remote_copy(
            src_ref=src, dst_ref=dst, send_sem=ssem, recv_sem=rsem,
            device_id=dev, device_id_type=MESH,
        )

    def piece(slot, h):
        return kv.at[slot, pl.ds(h * half, half)]

    def give(slot, h, dst, dev):
        copy = remote(piece(slot, h), piece(dst, h), ks.at[0], kr.at[dst, h], dev)
        copy.start()

    def got(slot, h):
        remote(piece(slot, h), piece(slot, h), ks.at[0], kr.at[slot, h], to_c).wait_recv()

    def chunk(m, h):
        return qq.at[m, pl.ds(h * half, half)]

    def ask(m, slot, h, sem, dev):
        return remote(chunk(m, h), chunk(slot, h), sem, qr.at[slot, h], dev)

    def got_chunk(m, h):
        ask(0, m, h, qs.at[0], to_c).wait_recv()

    def pass_on(m, h):
        @pl.when(inner == 1)
        def _():
            got_chunk(m, h)
            ask(m, 5 - m, h, qf.at[0], to_z(1)).start()

    give(0, 1, 1, to_x)
    give(0, 0, 2, to_y)
    give(0, 0, 1, to_x)
    give(0, 1, 2, to_y)
    for m in [1 + 2 * inner, 2 - inner] + list(range(4, zc)):
        for h in range(2):
            copy = ask(0, m, h, qs.at[0], to_z(m))
            copy.start()
    give(0, 0, 4, to_c)
    give(0, 1, 4, to_c)
    tables = [
        remote(lst.at[0], lst.at[1], bs.at[0], bs.at[1], to_x),
        remote(cnt.at[0], cnt.at[1], bs.at[2], bs.at[3], to_x),
    ]
    for copy in tables:
        copy.start()

    def mask_rows(side):
        blocks = lst.shape[2]
        shard_blocks = rows // BLK
        slab_blocks = 4 * shard_blocks
        ids = lst[side]
        local = ids // (shard_blocks * slabs) * shard_blocks + ids % shard_blocks
        used = lax.broadcasted_iota(jnp.int32, ids.shape, 0) < cnt[side]
        row = lax.broadcasted_iota(jnp.int32, (slab_blocks, blocks), 0)
        on = jnp.zeros((slab_blocks, blocks), jnp.float32)
        for g in range(slab_blocks):
            hit = jnp.max(jnp.where((local == g) & used, 1.0, 0.0), axis=0, keepdims=True)
            on = jnp.where(row == g, hit, on)
        spread = jnp.where(
            lax.broadcasted_iota(jnp.int32, (slab_blocks, 4 * rows), 1) // BLK
            == lax.broadcasted_iota(jnp.int32, (slab_blocks, 4 * rows), 0),
            1.0, 0.0,
        )
        full = lax.dot_general(
            on, spread, (((0,), (0,)), ((), ())), preferred_element_type=jnp.float32
        )
        full = (full - 1.0) * 1e30
        for g in range(blocks):
            for p in range(4):
                bias[side, g, p] = full[g : g + 1, p * rows : (p + 1) * rows]

    def partial(mask, pieces):
        zt = flip(z, mask, bits)
        best = None
        at = 0
        spans = []
        for r, h in pieces:
            pbr = flip(pb, (r // 2) % 2 * 2 + r // 4, 2)
            lo, hi = (0, rows) if h is None else (h * half, h * half + half)
            s = lax.dot_general(
                qq[mask, :, hd:], kv[r, lo:hi, 0:hd], NT, preferred_element_type=jnp.float32
            )
            s = jnp.concatenate(
                [
                    s[g * half : (g + 1) * half]
                    + bias[r % 2, (zt * 2 + x) * 2 + g, pbr][:, lo:hi]
                    for g in range(2)
                ],
                axis=0,
            )
            s_scr[:, at : at + hi - lo] = s
            for g in range(0, hi - lo, hd):
                top = s[:, g : g + hd]
                best = top if best is None else jnp.maximum(best, top)
            spans.append((r, lo, hi, at))
            at += hi - lo
        peak = jnp.max(best, axis=1, keepdims=True)
        total = slope = both = tang = None
        for r, lo, hi, at in spans:
            p = jnp.exp2((s_scr[:, at : at + hi - lo] - peak) * factor)
            t = lax.dot_general(
                qq[mask], kv[r, lo:hi, 0 : 2 * hd], NT, preferred_element_type=jnp.float32
            )
            pt = p * t
            p_scr[:, at : at + hi - lo] = p.astype(jnp.bfloat16)
            ps_scr[:, at : at + hi - lo] = pt.astype(jnp.bfloat16)
            for g in range(0, hi - lo, hd):
                p2, pt2 = p[:, g : g + hd], pt[:, g : g + hd]
                total = p2 if total is None else total + p2
                slope = pt2 if slope is None else slope + pt2
        total = jnp.sum(total, axis=1, keepdims=True)
        slope = jnp.sum(slope, axis=1, keepdims=True)
        for r, lo, hi, at in spans:
            a = jnp.dot(
                p_scr[:, at : at + hi - lo], kv[r, lo:hi, 2 * hd :],
                preferred_element_type=jnp.float32,
            )
            b = jnp.dot(
                ps_scr[:, at : at + hi - lo], kv[r, lo:hi, 2 * hd : 3 * hd],
                preferred_element_type=jnp.float32,
            )
            both = a if both is None else both + a
            tang = b if tang is None else tang + b
        return peak, total, slope, both[:, :hd], tang * scale + both[:, hd:]

    def close(peak, total, slope, weighted, tang):
        mean = slope * scale / total
        centred = tang - mean * weighted
        lane = lax.broadcasted_iota(jnp.int32, weighted.shape, 1)
        stats = jnp.where(lane == 0, peak, jnp.where(lane == 1, total, mean))
        return weighted, centred, stats.T[0:4]

    def pack(flat, other=None):
        other = flat[:, half:] if other is None else other
        return jnp.concatenate([flat[:, :half], other], axis=0)

    def join(a, b):
        peak = jnp.maximum(a[0], b[0])
        fa, fb = jnp.exp2((a[0] - peak) * factor), jnp.exp2((b[0] - peak) * factor)
        return (peak,) + tuple(fa * m + fb * n for m, n in zip(a[1:], b[1:]))

    low, high = slice(0, half), slice(half, rows)

    def result_copies(mask):
        dev = to_z(1) if isinstance(mask, int) and mask == 2 else to_z(mask)
        return (
            remote(send.at[mask], recv.at[mask], rs.at[0], rr.at[mask], dev),
            remote(sstat.at[mask], rstat.at[mask], ts.at[0], tr.at[mask], dev),
        )

    def put(slot, span, weighted, centred):
        send[slot, span, 0:hd] = weighted.astype(jnp.bfloat16)
        send[slot, span, hd:] = centred.astype(jnp.bfloat16)

    def hand_in(mask, weighted, centred, flat):
        put(mask, slice(None), weighted, centred)
        sstat[mask] = pack(flat)
        for copy in result_copies(mask):
            copy.start()

    def send_part(src, slot, span, stats, sem, dev):
        remote(send.at[src, span], recv.at[slot, span], rs.at[0], rr.at[slot], dev).start()
        if stats is not None:
            remote(sstat.at[stats], rstat.at[slot], sem, tr.at[slot], dev).start()

    def got_result(slot, span=slice(None)):
        for ref, sem in ((recv.at[slot, span], rr), (rstat.at[slot], tr)):
            remote(ref, ref, sem.at[slot], sem.at[slot], to_c).wait_recv()

    def cut(part, span):
        return tuple(a[span] for a in part)

    def arrived(slot, span):
        coef[0:4, :half], coef[0:4, half:] = rstat[slot, 0:4], rstat[slot, 4:8]
        cols = coef[:, span].T
        pk, tot, mean = cols[:, 0:1], cols[:, 1:2], cols[:, 2:3]
        w = recv[slot, span, 0:hd].astype(jnp.float32)
        d = recv[slot, span, hd:].astype(jnp.float32)
        return pk, tot, mean * tot / scale, w, d + mean * w

    def got_queries(mask):
        for h in range(2):
            got_chunk(mask, h)

    most = tuple((r, None) for r in (0, 1, 2, 4, 5, 6))
    last = ((3, None), (7, None))
    whole = most + last

    mask_rows(0)
    pass_on(3, 0)
    got(2, 0)
    give(2, 0, 3, to_x)
    give(2, 0, 6, to_c)
    got(1, 1)
    give(1, 1, 3, to_y)
    give(1, 1, 5, to_c)
    pass_on(3, 1)
    pass_on(2, 0)
    got(1, 0)
    give(1, 0, 5, to_c)
    got(2, 1)
    give(2, 1, 6, to_c)
    pass_on(2, 1)
    for copy in tables:
        copy.wait_recv()
    mask_rows(1)

    @pl.when(inner == 0)
    def _():
        got_queries(2)

    for slot in (4, 5, 6):
        for h in range(2):
            got(slot, h)
    second = partial(2, most)
    for h in range(2):
        got(3, h)
        give(3, h, 7, to_c)

    for h in range(2):
        got(7, h)
    coef[...] = jnp.zeros_like(coef)
    second = close(*join(second, partial(2, last)))

    @pl.when(inner == 0)
    def _():
        hand_in(2, *second)

    line = lax.broadcasted_iota(jnp.int32, (8, half), 0)

    @pl.when(inner == 1)
    def _():
        put(2, slice(None), *second[:2])
        stats = pack(second[2])
        sstat[zc] = stats
        sstat[2] = jnp.where((line < 4) | (line % 4 == 0), stats, 0.0)
        send_part(2, zc, high, zc, ts.at[1], to_z(3))
        send_part(2, 2, low, 2, ts.at[0], to_z(2))

    soon, later = 3 - 2 * inner, 1 + 2 * inner
    got_queries(soon)
    first = partial(soon, whole)
    near = close(*first)

    @pl.when(inner == 0)
    def _():
        hand_in(3, *near)

    @pl.when(inner == 1)
    def _():
        put(1, low, *cut(near[:2], low))
        send_part(1, 1, low, None, None, to_z(1))

    @pl.when(inner == 0)
    def _():
        got_queries(1)

    third = partial(later, whole)

    @pl.when(inner == 0)
    def _():
        hand_in(1, *close(*third))

    @pl.when(inner == 1)
    def _():
        got_result(zc, high)
        w, centred, flat = close(*join(cut(first, high), arrived(zc, high)))
        put(1, high, w, centred)
        sstat[1] = pack(near[2], flat)
        send_part(1, 1, high, 1, ts.at[0], to_z(1))

    def step(mask, carry):
        got_queries(mask)
        hand_in(mask, *close(*partial(mask, whole)))
        return carry

    if zc > 4:
        lax.fori_loop(4, zc, step, 0)
    own = partial(0, whole)
    own_w, own_c, own_flat = close(*own)
    recv[0, :, 0:hd] = own_w.astype(jnp.bfloat16)
    recv[0, :, hd:] = own_c.astype(jnp.bfloat16)
    rstat[0] = pack(own_flat)

    @pl.when(inner == 1)
    def _():
        got_result(2)
        hand_in(3, *close(*join(third, arrived(2, slice(None)))))
        recv[2] = jnp.zeros_like(recv[2])
        rstat[2] = jnp.where(line % 4 == 0, rstat[0], 0.0)
        coef[0:8, :] = jnp.zeros((8, rows), jnp.float32)

    @pl.when(inner == 0)
    def _():
        got_result(2, low)
        recv[2, half:] = jnp.zeros((half, 2 * hd), jnp.bfloat16)

    for m in [1, 3] + list(range(4, zc)):
        got_result(m)

    def stat(m, n):
        return jnp.concatenate([rstat[m, n : n + 1], rstat[m, n + 4 : n + 5]], axis=1)

    peaks = [stat(m, 0) for m in range(zc)]
    peak = functools.reduce(jnp.maximum, peaks)
    shares = [jnp.exp2((pk - peak) * factor) for pk in peaks]
    total = sum(a * stat(m, 1) for m, a in enumerate(shares))
    mean = sum(a * stat(m, 1) * stat(m, 2) for m, a in enumerate(shares)) / total
    for m, a in enumerate(shares):
        a = a / total
        coef[2 * m : 2 * m + 1, :] = a
        coef[2 * m + 1 : 2 * m + 2, :] = a * (stat(m, 2) - mean)
    columns = coef[...].T
    out = outt = 0.0
    for m in range(zc):
        w = recv[m, :, 0:hd].astype(jnp.float32)
        d = recv[m, :, hd:].astype(jnp.float32)
        a, g = columns[:, 2 * m : 2 * m + 1], columns[:, 2 * m + 1 : 2 * m + 2]
        out = out + a * w
        outt = outt + (a * d + g * w)
    out_ref[:, 0:hd] = out.astype(out_ref.dtype)
    out_ref[:, hd:] = outt.astype(out_ref.dtype)
    def all_sent(ref, sem):
        remote(ref, ref, sem, sem, to_c).wait_send()

    all_sent(kv.at[pl.ds(0, 7)], ks.at[0])
    all_sent(qq.at[pl.ds(0, 2 + max(zc - 4, 0))], qs.at[0])

    @pl.when(inner == 1)
    def _():
        all_sent(qq.at[pl.ds(0, 2)], qf.at[0])

    for copy in tables:
        copy.wait_send()
    all_sent(send.at[pl.ds(1, zc - 1)], rs.at[0])
    all_sent(sstat.at[pl.ds(1, zc - 1)], ts.at[0])

    @pl.when(inner == 1)
    def _():
        all_sent(sstat.at[0], ts.at[1])


def shards(
    queries, query_tangent, keys, values, key_tangent, value_tangent, block_list, block_count
):
    rows, hd = keys.shape
    slabs, pbs = lax.axis_size("kv"), lax.axis_size("pb")
    zc = slabs // 2
    list_t = block_list[:, 0, :].T
    count_t = block_count.T
    blocks = list_t.shape[1]
    vmem = pl.BlockSpec(memory_space=pltpu.VMEM)
    hbm = pl.BlockSpec(memory_space=pl.ANY)
    dma = pltpu.SemaphoreType.DMA
    out = pl.pallas_call(
        functools.partial(kernel, zc, slabs),
        out_shape=jax.ShapeDtypeStruct((rows, 2 * hd), jnp.bfloat16),
        in_specs=[hbm] * 8,
        out_specs=vmem,
        scratch_shapes=[
            pltpu.VMEM((8, rows, 4 * hd), jnp.bfloat16),
            pltpu.VMEM((zc, rows, 2 * hd), jnp.bfloat16),
            pltpu.VMEM((2,) + list_t.shape, jnp.int32),
            pltpu.VMEM((2, 1, blocks), jnp.int32),
            pltpu.VMEM((2, blocks, pbs, 1, rows), jnp.float32),
            pltpu.VMEM((rows, 8 * rows), jnp.float32),
            pltpu.VMEM((rows, 8 * rows), jnp.bfloat16),
            pltpu.VMEM((rows, 8 * rows), jnp.bfloat16),
            pltpu.VMEM((zc, rows, 2 * hd), jnp.bfloat16),
            pltpu.VMEM((zc + 1, 8, rows // 2), jnp.float32),
            pltpu.VMEM((zc + 1, rows, 2 * hd), jnp.bfloat16),
            pltpu.VMEM((zc + 1, 8, rows // 2), jnp.float32),
            pltpu.VMEM((128, rows), jnp.float32),
            dma((4,)),
            dma((1,)),
            dma((8, 2)),
            dma((1,)),
            dma((zc, 2)),
            dma((1,)),
            dma((4,)),
            dma((1,)),
            dma((zc + 1,)),
            dma((2,)),
            dma((zc + 1,)),
        ],
        compiler_params=pltpu.CompilerParams(
            collective_id=0, has_side_effects=True, vmem_limit_bytes=20 * 1024 * 1024
        ),
    )(*[pltpu.with_memory_space_constraint(a, pltpu.HBM) for a in (queries, query_tangent, keys, values, key_tangent, value_tangent, list_t, count_t)])
    return out[:, :hd], out[:, hd:]


def solution(mesh):
    rows = P(("pb", "kv"), None)
    return jax.shard_map(
        shards,
        mesh=mesh,
        in_specs=(rows,) * 6 + (P("pb", "kv", None), P("pb", "kv")),
        out_specs=(rows, rows),
        check_vma=False,
    )
```
